32 devices in a mesh: gx: 2 (over y), gy: 4 (over x, core), gz: 4 (over z).
Axes of the slice: x: 2, y: 2, z: 4, core: 2. Of those that a mesh axis runs over, the one named last changes fastest.
Arguments:
- midpoints: float32 [3, 2, 4, 4, 1024], P(None, 'gx', 'gy', 'gz'), may hold values from 0 to 1
- line_vectors: float32 [3, 2, 4, 4, 1024], P(None, 'gx', 'gy', 'gz'), may hold values from -0.085 to 0.085
- burgers: float32 [3, 2, 4, 4, 1024], P(None, 'gx', 'gy', 'gz'), may hold values from -1.7 to 1.7
- live_mask: int32 [2, 4, 4, 1024], P('gx', 'gy', 'gz'), may hold values from 0 to 1, as said below
- pair_list: int32 [13, 2, 4, 4], P(None, 'gx', 'gy', 'gz'), may hold values 0 or 1
Outputs:
- forces: float32 [3, 2, 4, 4, 1024], P(None, 'gx', 'gy', 'gz')
The draws below stay inside these ranges and needn't reach their ends.
Inputs may be any that keep to these rules, and one draw needn't show every extreme that they name: `live_mask`: the live slots of each cell are a prefix of its 1024 slots; every cell has at least 256 live slots, and some cell has all 1024 live.
All inputs are finite; a program needn't handle non-finite values. No bound on the sum of `pair_list` on one device may be relied on, other than what follows from the above.
Results may differ from the reference program's by a relative error of at most 0.0003.
Values sent between devices are 32-bit elements; how exact they have to be, the bound alone decides.
A program may use at most 64 MiB of HBM per device.

```python
import jax
import jax.numpy as jnp
from jax import lax

SEG = 1024
NX = 2
NY = 4
NZ = 4


def draw_line_vectors(key, part):
    base = jax.random.uniform(jax.random.fold_in(key, 11), (3, NX, NY, NZ, SEG), jnp.float32, -1.0, 1.0)
    common = jax.random.uniform(jax.random.fold_in(key, 12), (3, NX, NY, NZ, 1), jnp.float32, -0.7, 0.7)
    return 0.05 * (base + common)


def draw_burgers(key, part):
    base = jax.random.uniform(jax.random.fold_in(key, 21), (3, NX, NY, NZ, SEG), jnp.float32, -1.0, 1.0)
    common = jax.random.uniform(jax.random.fold_in(key, 22), (3, NX, NY, NZ, 1), jnp.float32, -0.7, 0.7)
    return base + common


def draw_live_mask(key, part):
    counts = jax.random.randint(jax.random.fold_in(key, 31), (NX, NY, NZ), SEG // 4, SEG + 1)
    chosen = jax.random.randint(jax.random.fold_in(key, 32), (), 0, NX * NY * NZ)
    cell_ids = jnp.arange(NX * NY * NZ, dtype=jnp.int32).reshape(NX, NY, NZ)
    counts = jnp.where(cell_ids == chosen, SEG, counts)
    slots = jnp.arange(SEG, dtype=jnp.int32)
    return (slots[None, None, None, :] < counts[..., None]).astype(jnp.int32)


def with_ends(entries, own_key, smallest, top_value):
    spot = [jax.random.randint(jax.random.fold_in(own_key, axis), (), 0, length) for axis, length in enumerate(entries.shape)]
    longest = entries.shape.index(max(entries.shape))
    next_to = spot[:longest] + [(spot[longest] + 1) % entries.shape[longest]] + spot[longest + 1:]
    return entries.at[tuple(spot)].set(smallest).at[tuple(next_to)].set(top_value)


def block_scale(rng, dims, pieces, smallest, high):
    factor_of, own = 1.0, jax.random.fold_in(rng, 6)
    for axis_at, parts in pieces:
        steps = jnp.exp(jax.random.uniform(jax.random.fold_in(own, axis_at), (parts,), jnp.float32, smallest / len(pieces), high / len(pieces)))
        factor_of = factor_of * jnp.repeat(steps, dims[axis_at] // parts).reshape([-1 if axis == axis_at else 1 for axis in range(len(dims))])
    return factor_of


def setup_inputs(seed: int = 0) -> dict:
    seeds = jax.random.split(jax.random.key(seed), 6)
    midpoints = jnp.clip(1.0 * jax.random.uniform(seeds[0], (3, NX, NY, NZ, SEG), jnp.float32) ** block_scale(seeds[0], (3, NX, NY, NZ, SEG), ((1, 2), (2, 4), (3, 4)), -0.2, 0.2), 0.0, 1.0)
    line_vectors = draw_line_vectors(jax.random.fold_in(seeds[5], 71), 0)
    burgers = draw_burgers(jax.random.fold_in(seeds[5], 71), 0)
    live_mask = draw_live_mask(jax.random.fold_in(seeds[5], 71), 0)
    pair_list = with_ends((jax.random.randint(seeds[4], (13, NX, NY, NZ), 0, 2) < 1).astype(jnp.int32), jax.random.fold_in(seeds[4], 1), 0, 1)
    return {"midpoints": midpoints, "line_vectors": line_vectors, "burgers": burgers, "live_mask": live_mask, "pair_list": pair_list}


CORE_WIDTH = 0.1
SPLIT_WIDTH = 2.0
HIGHEST = lax.Precision.HIGHEST
HALF_SHELL = [(step_x, step_y, step_z) for step_x in (-1, 0, 1) for step_y in (-1, 0, 1) for step_z in (-1, 0, 1) if (step_x, step_y, step_z) > (0, 0, 0)]

def pair_terms(target_mid, target_weight, source_mid, source_weight, offset, with_back):
    coupling = jnp.dot(target_weight.T, source_weight, precision=HIGHEST, preferred_element_type=jnp.float32)
    deltas = [target_mid[component][:, None] - source_mid[component][None, :] - float(offset[component]) for component in range(3)]
    squared = deltas[0] * deltas[0] + deltas[1] * deltas[1] + deltas[2] * deltas[2]
    inner_inv = lax.rsqrt(squared + CORE_WIDTH * CORE_WIDTH)
    outer_inv = lax.rsqrt(squared + SPLIT_WIDTH * SPLIT_WIDTH)
    strength = coupling * (inner_inv * inner_inv * inner_inv - outer_inv * outer_inv * outer_inv)
    forward = jnp.stack([lax.optimization_barrier(jnp.sum(strength * delta_part, axis=1)) for delta_part in deltas])
    if with_back:
        backward = -jnp.stack([lax.optimization_barrier(jnp.sum(strength * delta_part, axis=0)) for delta_part in deltas])
        return (forward, backward)
    return forward

def cell_moments(weights, middle, cell_coords):
    offset_rows = [middle[component] + (cell_coords[component] % 2).astype(jnp.float32) - 1.0 for component in range(3)]
    moment_basis = [jnp.ones_like(middle[0])] + offset_rows + [offset_rows[first] * offset_rows[second] for first in range(3) for second in range(3)]
    return jnp.dot(weights, jnp.stack(moment_basis).T, precision=HIGHEST, preferred_element_type=jnp.float32)

def far_field(coarse_table, weights, middle, cell_coords, fine_dims, coarse_dims):
    coarse_count = coarse_dims[0] * coarse_dims[1] * coarse_dims[2]
    coarse_index = jnp.arange(coarse_count, dtype=jnp.int32)
    coarse_coords = (coarse_index // (coarse_dims[1] * coarse_dims[2]), coarse_index // coarse_dims[2] % coarse_dims[1], coarse_index % coarse_dims[2])
    displace = []
    for component in range(3):
        cell_gap = cell_coords[component] - 2 * coarse_coords[component]
        cell_gap = (cell_gap + fine_dims[component] // 2) % fine_dims[component] - fine_dims[component] // 2
        displace.append(cell_gap.astype(jnp.float32)[:, None] + middle[component][None, :] - 1.0)
    spread = jnp.stack(displace)
    weighted = jnp.einsum('kcq,ci->qki', coarse_table.reshape(coarse_count, 9, 13), weights, precision=HIGHEST)
    monopole = weighted[0]
    dipole = weighted[1:4]
    quadrupole = weighted[4:13].reshape(3, 3, coarse_count, weights.shape[1])
    inv_radius = lax.rsqrt(lax.optimization_barrier(jnp.sum(spread * spread, axis=0)) + SPLIT_WIDTH * SPLIT_WIDTH)
    inv_cube = inv_radius * inv_radius * inv_radius
    inv_fifth = inv_cube * inv_radius * inv_radius
    inv_seventh = inv_fifth * inv_radius * inv_radius
    dipole_dot = lax.optimization_barrier(jnp.sum(dipole * spread, axis=0))
    quad_dot = lax.optimization_barrier(jnp.sum(quadrupole * spread[None], axis=1))
    quad_form = lax.optimization_barrier(jnp.sum(spread * quad_dot, axis=0))
    quad_trace = quadrupole[0, 0] + quadrupole[1, 1] + quadrupole[2, 2]
    radial = -monopole * inv_cube - 3.0 * dipole_dot * inv_fifth - 7.5 * quad_form * inv_seventh + 1.5 * quad_trace * inv_fifth
    gradient = spread * radial[None] + dipole * inv_cube[None] + 3.0 * quad_dot * inv_fifth[None]
    return -lax.optimization_barrier(jnp.sum(gradient, axis=1))

def reference(midpoints, line_vectors, burgers, live_mask, pair_list):
    cell_count = NX * NY * NZ
    alive_mask = live_mask.astype(jnp.float32)
    masked_line = line_vectors * alive_mask[None]
    weights = (burgers[:, None] * masked_line[None]).reshape(9, NX, NY, NZ, SEG)

    def to_rows(cell_grid):
        return jnp.moveaxis(cell_grid, 0, 3).reshape(cell_count, cell_grid.shape[0], SEG)

    def to_grid(row_array):
        return jnp.moveaxis(row_array.reshape(NX, NY, NZ, 3, SEG), 3, 0)
    flat_mid = to_rows(midpoints)
    flat_weight = to_rows(weights)
    summed = to_grid(lax.map(lambda record: pair_terms(record[0], record[1], record[0], record[1], (0, 0, 0), False), (flat_mid, flat_weight)))
    for offset_index, offset in enumerate(HALF_SHELL):
        back_shift = (-offset[0], -offset[1], -offset[2])
        source_mid = to_rows(jnp.roll(midpoints, back_shift, axis=(1, 2, 3)))
        source_weight = to_rows(jnp.roll(weights, back_shift, axis=(1, 2, 3)))
        pair_flags = pair_list[offset_index].reshape(cell_count)

        def one_pair(record, offset=offset):
            zeros_block = jnp.zeros((3, SEG), midpoints.dtype)
            return lax.cond(record[4] > 0, lambda: pair_terms(record[0], record[1], record[2], record[3], offset, True), lambda: (zeros_block, zeros_block))
        forward, backward = lax.map(one_pair, (flat_mid, flat_weight, source_mid, source_weight, pair_flags))
        summed = summed + to_grid(forward) + jnp.roll(to_grid(backward), offset, axis=(1, 2, 3))
    grid_ids = jnp.arange(cell_count, dtype=jnp.int32)
    coord_x = grid_ids // (NY * NZ)
    coord_y = grid_ids // NZ % NY
    coord_z = grid_ids % NZ
    moments = lax.map(lambda record: cell_moments(record[0], record[1], (record[2], record[3], record[4])), (flat_weight, flat_mid, coord_x, coord_y, coord_z))
    coarse_table = moments.reshape(NX // 2, 2, NY // 2, 2, NZ // 2, 2, 117).sum(axis=(1, 3, 5)).reshape(-1, 117)
    coarse_dims = (NX // 2, NY // 2, NZ // 2)
    far = lax.map(lambda record: far_field(coarse_table, record[0], record[1], (record[2], record[3], record[4]), (NX, NY, NZ), coarse_dims), (flat_weight, flat_mid, coord_x, coord_y, coord_z))
    return (summed + to_grid(far)) * alive_mask[None]
```

```python
import functools

import jax
import jax.numpy as jnp
from jax import lax
from jax.experimental import pallas as pl
from jax.experimental.pallas import tpu as pltpu
from jax.sharding import PartitionSpec as P

AXES = ("gx", "gy", "gz")
CORE_SQ = 0.1 * 0.1
SPLIT_SQ = 2.0 * 2.0
TI = 256
TJ = 256
ROWS = 64
F32 = jnp.float32
BF16 = jnp.bfloat16
NT = (((1,), (1,)), ((), ()))


def reps(size):
    return [0] if size == 1 else [0, 1] if size == 2 else [0, 1, -1]


def cell_id(cell, dims):
    return (cell[0] * dims[1] + cell[1]) * dims[2] + cell[2]


def gather_kernel(dims, mid_ref, line_ref, burg_ref, live_ref, pair_ref, blocks, ctrl,
                  weights, basis, send_sem, recv_sem, csend_sem, crecv_sem):
    me = tuple(lax.axis_index(a) for a in AXES)
    my_id = cell_id(me, dims)
    count = dims[0] * dims[1] * dims[2]
    barrier = pltpu.get_barrier_semaphore()

    def coords(other):
        return (other // (dims[1] * dims[2]), other // dims[2] % dims[1], other % dims[2])

    def greet(step, carry):
        pl.semaphore_signal(barrier, inc=1, device_id=coords((my_id + step) % count),
                            device_id_type=pl.DeviceIdType.MESH)
        return carry

    lax.fori_loop(1, count, greet, 0)

    alive = live_ref[...].astype(F32)
    line, burg, mid = [], [], []
    for c in range(3):
        mid.append(mid_ref[c])
        line.append(line_ref[c] * alive)
        burg.append(burg_ref[c])
        blocks[0, c] = mid[c]
        blocks[0, 3 + c] = line[c]
        blocks[0, 6 + c] = burg[c]
    basis[...] = jnp.zeros_like(basis)
    weights[...] = jnp.zeros_like(weights)
    z = [mid[c] + ((me[c] % 2) - 1).astype(F32) for c in range(3)]
    rows = [jnp.ones_like(z[0])] + z + [z[a] * z[b] for a in range(3) for b in range(3)]
    for q in range(13):
        basis[q:q + 1] = rows[q]
    for a in range(3):
        for b in range(3):
            weights[3 * a + b:3 * a + b + 1] = burg[a] * line[b]
    moments = lax.dot_general(weights[...], basis[...], NT, precision=lax.Precision.HIGHEST,
                              preferred_element_type=F32)
    sub = lax.broadcasted_iota(jnp.int32, moments.shape, 0)
    flat = jnp.where(sub == 0, moments, 0.0)
    for c in range(1, 9):
        flat = flat + pltpu.roll(jnp.where(sub == c, moments, 0.0), 13 * c, 1)
    ctrl[my_id, 0:1] = jnp.sum(flat, axis=0, keepdims=True)
    lane = lax.broadcasted_iota(jnp.int32, (1, 128), 1)
    flags = jnp.where(lane == 13, jnp.sum(alive, axis=1, keepdims=True), 0.0)
    for k in range(13):
        flags = flags + jnp.where(lane == k, pair_ref[k].astype(F32), 0.0)
    ctrl[my_id, 1:2] = flags

    pl.semaphore_wait(barrier, count - 1)

    grid = [(x, y, w) for x in reps(dims[0]) for y in reps(dims[1]) for w in reps(dims[2])]
    copies = []
    for slot, rep in enumerate(grid):
        if slot == 0:
            continue
        to = tuple((me[i] - rep[i] + dims[i]) % dims[i] for i in range(3))
        copy = pltpu.make_async_remote_copy(
            src_ref=blocks.at[0], dst_ref=blocks.at[slot], send_sem=send_sem.at[slot],
            recv_sem=recv_sem.at[slot], device_id=to, device_id_type=pl.DeviceIdType.MESH)
        copy.start()
        copies.append(copy)

    def ctrl_copy(step):
        return pltpu.make_async_remote_copy(
            src_ref=ctrl.at[my_id], dst_ref=ctrl.at[my_id], send_sem=csend_sem.at[step],
            recv_sem=crecv_sem.at[step], device_id=coords((my_id + step) % count),
            device_id_type=pl.DeviceIdType.MESH)

    def send_ctrl(step, carry):
        ctrl_copy(step).start()
        return carry

    lax.fori_loop(1, count, send_ctrl, 0)

    def wait_ctrl(step, carry):
        ctrl_copy(step).wait()
        return carry

    lax.fori_loop(1, count, wait_ctrl, 0)
    for copy in copies:
        copy.wait()


def split3(value):
    high = value.astype(BF16).astype(F32)
    rest = value - high
    middle = rest.astype(BF16).astype(F32)
    return high, middle, rest - middle


def force_kernel(dims, scalars, blocks, ctrl, mid8, line8, burg8, live8, out,
                 feat, wide, tall, target, source_q, source_w, force, coarse, coarse_s, sem):
    me = tuple(lax.axis_index(a) for a in AXES)
    my_id = cell_id(me, dims)
    seg = blocks.shape[3]
    kdims = tuple(d // 2 for d in dims)
    kcount = kdims[0] * kdims[1] * kdims[2]

    def coarse_sum(k, carry):
        kx, ky, kz = k // (kdims[1] * kdims[2]), k // kdims[2] % kdims[1], k % kdims[2]
        total = jnp.zeros((1, 128), F32)
        for a in range(2):
            for b in range(2):
                for c in range(2):
                    total = total + ctrl[cell_id((2 * kx + a, 2 * ky + b, 2 * kz + c), dims), 0:1]
        coarse[k] = total
        return carry

    lax.fori_loop(0, kcount, coarse_sum, 0)
    table = pltpu.make_async_copy(coarse, coarse_s, sem)
    table.start()

    feat[...] = jnp.zeros_like(feat)
    wide[...] = jnp.zeros_like(wide)
    tall[...] = jnp.zeros_like(tall)
    force[...] = jnp.zeros_like(force)

    def fill_weights(slot):
        for a in range(3):
            for b in range(3):
                wide[3 * a + b:3 * a + b + 1] = blocks[slot, 6 + a] * blocks[slot, 3 + b]

    ones = jnp.ones((1, seg), F32)
    x = [blocks[0, c] - 0.5 for c in range(3)]
    for c in range(3):
        feat[c:c + 1] = -2.0 * x[c]
    feat[3:4] = ones
    feat[4:5] = x[0] * x[0] + x[1] * x[1] + x[2] * x[2] + CORE_SQ
    high, middle, low = split3(feat[...])
    for at, part in enumerate((high, high, high, middle, middle, low)):
        tall[8 * at:8 * at + 8] = part
    fill_weights(0)
    whole = wide[...]
    whigh = whole.astype(BF16).astype(F32)
    tall[48:64] = whigh
    tall[64:80] = whigh
    tall[80:96] = whole - whigh
    target[...] = jnp.transpose(tall[...]).astype(BF16)

    def slot_of(offset):
        slot = 0
        for i in range(3):
            base = min(dims[i], 3)
            slot = slot * base + (offset[i] + base) % base
        return slot

    own_tiles = (scalars[my_id, 1, 13].astype(jnp.int32) + (TI - 1)) // TI

    def one_source(t, carry):
        offset = (t // 9 - 1, t // 3 % 3 - 1, t % 3 - 1)
        source_id = cell_id(tuple((me[i] + offset[i] + dims[i]) % dims[i] for i in range(3)), dims)
        ahead = t > 13
        flag = scalars[jnp.where(ahead, my_id, source_id), 1,
                       jnp.where(ahead, t - 14, jnp.maximum(12 - t, 0))]

        @pl.when(jnp.logical_or(t == 13, flag > 0.0))
        def _():
            slot = slot_of(offset)
            y = [blocks[slot, c] + (offset[c].astype(F32) - 0.5) for c in range(3)]
            for c in range(3):
                feat[c:c + 1] = y[c]
            feat[3:4] = y[0] * y[0] + y[1] * y[1] + y[2] * y[2]
            feat[4:5] = ones
            high, middle, low = split3(feat[...])
            source_q[0:16] = jnp.concatenate([high, middle], axis=0).astype(BF16)
            source_q[16:32] = jnp.concatenate([low, high], axis=0).astype(BF16)
            source_q[32:48] = jnp.concatenate([middle, high], axis=0).astype(BF16)
            fill_weights(slot)
            whole = wide[...]
            whigh = whole.astype(BF16)
            source_w[0:16] = whigh
            source_w[16:32] = (whole - whigh.astype(F32)).astype(BF16)
            source_w[32:48] = whigh
            tiles = (scalars[source_id, 1, 13].astype(jnp.int32) + (TJ - 1)) // TJ

            def source_tile(j, carry):
                cols = pl.ds(pl.multiple_of(j * TJ, TJ), TJ)
                q = source_q[:, cols]
                w = source_w[:, cols]

                def target_tile(i, carry):
                    base = pl.multiple_of(i * TI, TI)
                    for r in range(0, TI, ROWS):
                        rows = pl.ds(base + r, ROWS)
                        lhs = target[rows, :]
                        near = jnp.dot(lhs[:, 0:48], q, preferred_element_type=F32)
                        pull = jnp.dot(lhs[:, 48:96], w, preferred_element_type=F32)
                        inner = lax.rsqrt(near)
                        outer = lax.rsqrt(near + (SPLIT_SQ - CORE_SQ))
                        strength = pull * (inner * inner * inner - outer * outer * outer)
                        top = strength.astype(BF16)
                        rest = (strength - top.astype(F32)).astype(BF16)
                        force[rows, 0:32] += (
                            lax.dot_general(top, q[0:32], NT, preferred_element_type=F32)
                            + lax.dot_general(rest, q[0:32], NT, preferred_element_type=F32))
                    return carry

                return lax.fori_loop(0, own_tiles, target_tile, carry)

            lax.fori_loop(0, tiles, source_tile, 0)

        return carry

    lax.fori_loop(0, 27, one_source, 0)
    turned = jnp.transpose(force[...])
    near = [x[c] * turned[4:5] - (turned[c:c + 1] + turned[8 + c:9 + c] + turned[16 + c:17 + c])
            for c in range(3)]

    table.wait()
    alive = live8[...].astype(F32)
    w8 = [burg8[a] * (line8[b] * alive) for a in range(3) for b in range(3)]

    def far_step(k, grads):
        kc = (k // (kdims[1] * kdims[2]), k // kdims[2] % kdims[1], k % kdims[2])
        u = []
        for i in range(3):
            gap = (me[i] - 2 * kc[i] + dims[i] + dims[i] // 2) % dims[i] - dims[i] // 2
            u.append(mid8[i] + (gap.astype(F32) - 1.0))
        q = []
        for m in range(13):
            value = coarse_s[k, 0, m] * w8[0]
            for c in range(1, 9):
                value = value + coarse_s[k, 0, 13 * c + m] * w8[c]
            q.append(value)
        inv = lax.rsqrt(u[0] * u[0] + u[1] * u[1] + u[2] * u[2] + SPLIT_SQ)
        inv2 = inv * inv
        inv3 = inv2 * inv
        inv5 = inv3 * inv2
        inv7 = inv5 * inv2
        dip = q[1] * u[0] + q[2] * u[1] + q[3] * u[2]
        quad = [q[4 + 3 * a] * u[0] + q[5 + 3 * a] * u[1] + q[6 + 3 * a] * u[2] for a in range(3)]
        form = quad[0] * u[0] + quad[1] * u[1] + quad[2] * u[2]
        trace = q[4] + q[8] + q[12]
        radial = (1.5 * trace - 3.0 * dip) * inv5 - q[0] * inv3 - 7.5 * form * inv7
        return tuple(grads[c] + u[c] * radial + q[1 + c] * inv3 + 3.0 * quad[c] * inv5
                     for c in range(3))

    zero = jnp.zeros((8, seg // 8), F32)
    grads = lax.fori_loop(0, kcount, far_step, (zero, zero, zero))
    width = seg // 8
    for c in range(3):
        for s in range(8):
            cut = slice(s * width, (s + 1) * width)
            out[c, :, cut] = (near[c][:, cut] - grads[c][s:s + 1]) * alive[s:s + 1]


def on_device(dims, midpoints, line_vectors, burgers, live_mask, pair_list):
    seg = midpoints.shape[4]
    count = dims[0] * dims[1] * dims[2]
    kcount = count // 8
    slots = len(reps(dims[0])) * len(reps(dims[1])) * len(reps(dims[2]))
    mid, line, burg = (a.reshape(3, 1, seg) for a in (midpoints, line_vectors, burgers))
    vmem = pl.BlockSpec(memory_space=pltpu.VMEM)
    smem = pl.BlockSpec(memory_space=pltpu.SMEM)
    blocks, ctrl = pl.pallas_call(
        functools.partial(gather_kernel, dims),
        out_shape=(jax.ShapeDtypeStruct((slots, 9, 1, seg), F32),
                   jax.ShapeDtypeStruct((count, 2, 128), F32)),
        in_specs=[vmem] * 5,
        out_specs=(vmem, vmem),
        scratch_shapes=[
            pltpu.VMEM((16, seg), F32),
            pltpu.VMEM((128, seg), F32),
            pltpu.SemaphoreType.DMA((slots,)),
            pltpu.SemaphoreType.DMA((slots,)),
            pltpu.SemaphoreType.DMA((count,)),
            pltpu.SemaphoreType.DMA((count,)),
        ],
        compiler_params=pltpu.CompilerParams(collective_id=0, has_side_effects=True),
        name="gather",
    )(mid, line, burg, live_mask.reshape(1, seg), pair_list.reshape(13, 1, 1))
    eight = [a.reshape(3, 8, seg // 8) for a in (midpoints, line_vectors, burgers)]
    out = pl.pallas_call(
        functools.partial(force_kernel, dims),
        out_shape=jax.ShapeDtypeStruct((3, 1, seg), F32),
        in_specs=[smem] + [vmem] * 6,
        out_specs=vmem,
        scratch_shapes=[
            pltpu.VMEM((8, seg), F32),
            pltpu.VMEM((16, seg), F32),
            pltpu.VMEM((128, seg), F32),
            pltpu.VMEM((seg, 128), BF16),
            pltpu.VMEM((48, seg), BF16),
            pltpu.VMEM((48, seg), BF16),
            pltpu.VMEM((seg, 128), F32),
            pltpu.VMEM((kcount, 1, 128), F32),
            pltpu.SMEM((kcount, 1, 128), F32),
            pltpu.SemaphoreType.DMA,
        ],
        name="forces",
    )(ctrl, blocks, ctrl, *eight, live_mask.reshape(8, seg // 8))
    return out.reshape(3, 1, 1, 1, seg)


def solution(mesh):
    dims = tuple(mesh.shape[a] for a in AXES)
    placed = (
        P(None, "gx", "gy", "gz", None),
        P(None, "gx", "gy", "gz", None),
        P(None, "gx", "gy", "gz", None),
        P("gx", "gy", "gz", None),
        P(None, "gx", "gy", "gz"),
    )
    return jax.shard_map(
        functools.partial(on_device, dims),
        mesh=mesh,
        in_specs=placed,
        out_specs=P(None, "gx", "gy", "gz", None),
        check_vma=False,
    )
```

```python
import functools

import jax
import jax.numpy as jnp
from jax import lax
from jax.experimental import pallas as pl
from jax.experimental.pallas import tpu as pltpu
from jax.sharding import PartitionSpec as P

AXES = ("gx", "gy", "gz")
CORE_SQ = 0.1 * 0.1
SPLIT_SQ = 2.0 * 2.0
TI = 256
TJ = 256
F32 = jnp.float32
BF16 = jnp.bfloat16
NT = (((1,), (1,)), ((), ()))


def reps(size):
    return [0] if size == 1 else [0, 1] if size == 2 else [0, 1, -1]


def cell_id(cell, dims):
    return (cell[0] * dims[1] + cell[1]) * dims[2] + cell[2]


def gather_kernel(dims, mid_ref, line_ref, burg_ref, live_ref, pair_ref, blocks, ctrl,
                  weights, basis, send_sem, recv_sem, csend_sem, crecv_sem):
    me = tuple(lax.axis_index(a) for a in AXES)
    my_id = cell_id(me, dims)
    count = dims[0] * dims[1] * dims[2]
    barrier = pltpu.get_barrier_semaphore()

    def coords(other):
        return (other // (dims[1] * dims[2]), other // dims[2] % dims[1], other % dims[2])

    def greet(step, carry):
        pl.semaphore_signal(barrier, inc=1, device_id=coords((my_id + step) % count),
                            device_id_type=pl.DeviceIdType.MESH)
        return carry

    lax.fori_loop(1, count, greet, 0)

    alive = live_ref[...].astype(F32)
    line, burg, mid = [], [], []
    for c in range(3):
        mid.append(mid_ref[c])
        line.append(line_ref[c] * alive)
        burg.append(burg_ref[c])
        blocks[0, c] = mid[c]
        blocks[0, 3 + c] = line[c]
        blocks[0, 6 + c] = burg[c]
    basis[...] = jnp.zeros_like(basis)
    weights[...] = jnp.zeros_like(weights)
    z = [mid[c] + ((me[c] % 2) - 1).astype(F32) for c in range(3)]
    rows = [jnp.ones_like(z[0])] + z + [z[a] * z[b] for a in range(3) for b in range(3)]
    for q in range(13):
        basis[q:q + 1] = rows[q]
    for a in range(3):
        for b in range(3):
            weights[3 * a + b:3 * a + b + 1] = burg[a] * line[b]
    moments = lax.dot_general(weights[...], basis[...], NT, precision=lax.Precision.HIGHEST,
                              preferred_element_type=F32)
    sub = lax.broadcasted_iota(jnp.int32, moments.shape, 0)
    flat = jnp.where(sub == 0, moments, 0.0)
    for c in range(1, 9):
        flat = flat + pltpu.roll(jnp.where(sub == c, moments, 0.0), 13 * c, 1)
    ctrl[my_id, 0:1] = jnp.sum(flat, axis=0, keepdims=True)
    lane = lax.broadcasted_iota(jnp.int32, (1, 128), 1)
    flags = jnp.where(lane == 13, jnp.sum(alive, axis=1, keepdims=True), 0.0)
    for k in range(13):
        flags = flags + jnp.where(lane == k, pair_ref[k].astype(F32), 0.0)
    ctrl[my_id, 1:2] = flags

    pl.semaphore_wait(barrier, count - 1)

    grid = [(x, y, w) for x in reps(dims[0]) for y in reps(dims[1]) for w in reps(dims[2])]
    copies = []
    for slot, rep in enumerate(grid):
        if slot == 0:
            continue
        to = tuple((me[i] - rep[i] + dims[i]) % dims[i] for i in range(3))
        copy = pltpu.make_async_remote_copy(
            src_ref=blocks.at[0], dst_ref=blocks.at[slot], send_sem=send_sem.at[slot],
            recv_sem=recv_sem.at[slot], device_id=to, device_id_type=pl.DeviceIdType.MESH)
        copy.start()
        copies.append(copy)

    def ctrl_copy(step):
        return pltpu.make_async_remote_copy(
            src_ref=ctrl.at[my_id], dst_ref=ctrl.at[my_id], send_sem=csend_sem.at[step],
            recv_sem=crecv_sem.at[step], device_id=coords((my_id + step) % count),
            device_id_type=pl.DeviceIdType.MESH)

    def send_ctrl(step, carry):
        ctrl_copy(step).start()
        return carry

    lax.fori_loop(1, count, send_ctrl, 0)

    def wait_ctrl(step, carry):
        ctrl_copy(step).wait()
        return carry

    lax.fori_loop(1, count, wait_ctrl, 0)
    for copy in copies:
        copy.wait()


def split3(value):
    high = value.astype(BF16).astype(F32)
    rest = value - high
    middle = rest.astype(BF16).astype(F32)
    return high, middle, rest - middle


def force_kernel(dims, scalars, blocks, ctrl, mid8, line8, burg8, live8, out,
                 feat, wide, tall, target, source_q, source_w, force, coarse, coarse_s, sem):
    me = tuple(lax.axis_index(a) for a in AXES)
    my_id = cell_id(me, dims)
    seg = blocks.shape[3]
    kdims = tuple(d // 2 for d in dims)
    kcount = kdims[0] * kdims[1] * kdims[2]

    def coarse_sum(k, carry):
        kx, ky, kz = k // (kdims[1] * kdims[2]), k // kdims[2] % kdims[1], k % kdims[2]
        total = jnp.zeros((1, 128), F32)
        for a in range(2):
            for b in range(2):
                for c in range(2):
                    total = total + ctrl[cell_id((2 * kx + a, 2 * ky + b, 2 * kz + c), dims), 0:1]
        coarse[k] = total
        return carry

    lax.fori_loop(0, kcount, coarse_sum, 0)
    table = pltpu.make_async_copy(coarse, coarse_s, sem)
    table.start()

    feat[...] = jnp.zeros_like(feat)
    wide[...] = jnp.zeros_like(wide)
    tall[...] = jnp.zeros_like(tall)
    force[...] = jnp.zeros_like(force)

    def fill_weights(slot):
        for a in range(3):
            for b in range(3):
                wide[3 * a + b:3 * a + b + 1] = blocks[slot, 6 + a] * blocks[slot, 3 + b]

    ones = jnp.ones((1, seg), F32)
    x = [blocks[0, c] - 0.5 for c in range(3)]
    for c in range(3):
        feat[c:c + 1] = -2.0 * x[c]
    feat[3:4] = ones
    feat[4:5] = x[0] * x[0] + x[1] * x[1] + x[2] * x[2] + CORE_SQ
    high, middle, low = split3(feat[...])
    for at, part in enumerate((high, high, high, middle, middle, low)):
        tall[8 * at:8 * at + 8] = part
    fill_weights(0)
    whole = wide[...]
    whigh = whole.astype(BF16).astype(F32)
    tall[48:64] = whigh
    tall[64:80] = whigh
    tall[80:96] = whole - whigh
    target[...] = jnp.transpose(tall[...]).astype(BF16)

    def slot_of(offset):
        slot = 0
        for i in range(3):
            base = min(dims[i], 3)
            slot = slot * base + (offset[i] + base) % base
        return slot

    own_tiles = (scalars[my_id, 1, 13].astype(jnp.int32) + (TI - 1)) // TI

    def one_source(t, carry):
        offset = (t // 9 - 1, t // 3 % 3 - 1, t % 3 - 1)
        source_id = cell_id(tuple((me[i] + offset[i] + dims[i]) % dims[i] for i in range(3)), dims)
        ahead = t > 13
        flag = scalars[jnp.where(ahead, my_id, source_id), 1,
                       jnp.where(ahead, t - 14, jnp.maximum(12 - t, 0))]

        @pl.when(jnp.logical_or(t == 13, flag > 0.0))
        def _():
            slot = slot_of(offset)
            y = [blocks[slot, c] + (offset[c].astype(F32) - 0.5) for c in range(3)]
            for c in range(3):
                feat[c:c + 1] = y[c]
            feat[3:4] = y[0] * y[0] + y[1] * y[1] + y[2] * y[2]
            feat[4:5] = ones
            high, middle, low = split3(feat[...])
            source_q[0:16] = jnp.concatenate([high, middle], axis=0).astype(BF16)
            source_q[16:32] = jnp.concatenate([low, high], axis=0).astype(BF16)
            source_q[32:48] = jnp.concatenate([middle, high], axis=0).astype(BF16)
            fill_weights(slot)
            whole = wide[...]
            whigh = whole.astype(BF16)
            source_w[0:16] = whigh
            source_w[16:32] = (whole - whigh.astype(F32)).astype(BF16)
            source_w[32:48] = whigh
            tiles = (scalars[source_id, 1, 13].astype(jnp.int32) + (TJ - 1)) // TJ

            def source_tile(span, j, carry):
                cols = pl.ds(pl.multiple_of(j * TJ, TJ), TJ)
                q = source_q[:, cols]
                w = source_w[:, cols]

                lhs = target[0:span, :]
                near = jnp.dot(lhs[:, 0:48], q, preferred_element_type=F32)
                pull = jnp.dot(lhs[:, 48:96], w, preferred_element_type=F32)
                inner = lax.rsqrt(near)
                outer = lax.rsqrt(near + (SPLIT_SQ - CORE_SQ))
                strength = pull * (inner * inner * inner - outer * outer * outer)
                top = strength.astype(BF16)
                rest = (strength - top.astype(F32)).astype(BF16)
                force[0:span, 0:32] += (
                    lax.dot_general(top, q[0:32], NT, preferred_element_type=F32)
                    + lax.dot_general(rest, q[0:32], NT, preferred_element_type=F32))
                return carry

            for parts in range(1, seg // TI + 1):
                @pl.when(own_tiles == parts)
                def _(parts=parts):
                    lax.fori_loop(0, tiles, functools.partial(source_tile, parts * TI), 0)

        return carry

    lax.fori_loop(0, 27, one_source, 0)
    turned = jnp.transpose(force[...])
    near = [x[c] * turned[4:5] - (turned[c:c + 1] + turned[8 + c:9 + c] + turned[16 + c:17 + c])
            for c in range(3)]

    table.wait()
    alive = live8[...].astype(F32)
    w8 = [burg8[a] * (line8[b] * alive) for a in range(3) for b in range(3)]

    def far_step(k, grads):
        kc = (k // (kdims[1] * kdims[2]), k // kdims[2] % kdims[1], k % kdims[2])
        u = []
        for i in range(3):
            gap = (me[i] - 2 * kc[i] + dims[i] + dims[i] // 2) % dims[i] - dims[i] // 2
            u.append(mid8[i] + (gap.astype(F32) - 1.0))
        q = []
        for m in range(13):
            value = coarse_s[k, 0, m] * w8[0]
            for c in range(1, 9):
                value = value + coarse_s[k, 0, 13 * c + m] * w8[c]
            q.append(value)
        inv = lax.rsqrt(u[0] * u[0] + u[1] * u[1] + u[2] * u[2] + SPLIT_SQ)
        inv2 = inv * inv
        inv3 = inv2 * inv
        inv5 = inv3 * inv2
        inv7 = inv5 * inv2
        dip = q[1] * u[0] + q[2] * u[1] + q[3] * u[2]
        quad = [q[4 + 3 * a] * u[0] + q[5 + 3 * a] * u[1] + q[6 + 3 * a] * u[2] for a in range(3)]
        form = quad[0] * u[0] + quad[1] * u[1] + quad[2] * u[2]
        trace = q[4] + q[8] + q[12]
        radial = (1.5 * trace - 3.0 * dip) * inv5 - q[0] * inv3 - 7.5 * form * inv7
        return tuple(grads[c] + u[c] * radial + q[1 + c] * inv3 + 3.0 * quad[c] * inv5
                     for c in range(3))

    zero = jnp.zeros((8, seg // 8), F32)
    grads = lax.fori_loop(0, kcount, far_step, (zero, zero, zero))
    width = seg // 8
    for c in range(3):
        for s in range(8):
            cut = slice(s * width, (s + 1) * width)
            out[c, :, cut] = (near[c][:, cut] - grads[c][s:s + 1]) * alive[s:s + 1]


def on_device(dims, midpoints, line_vectors, burgers, live_mask, pair_list):
    seg = midpoints.shape[4]
    count = dims[0] * dims[1] * dims[2]
    kcount = count // 8
    slots = len(reps(dims[0])) * len(reps(dims[1])) * len(reps(dims[2]))
    mid, line, burg = (a.reshape(3, 1, seg) for a in (midpoints, line_vectors, burgers))
    vmem = pl.BlockSpec(memory_space=pltpu.VMEM)
    smem = pl.BlockSpec(memory_space=pltpu.SMEM)
    blocks, ctrl = pl.pallas_call(
        functools.partial(gather_kernel, dims),
        out_shape=(jax.ShapeDtypeStruct((slots, 9, 1, seg), F32),
                   jax.ShapeDtypeStruct((count, 2, 128), F32)),
        in_specs=[vmem] * 5,
        out_specs=(vmem, vmem),
        scratch_shapes=[
            pltpu.VMEM((16, seg), F32),
            pltpu.VMEM((128, seg), F32),
            pltpu.SemaphoreType.DMA((slots,)),
            pltpu.SemaphoreType.DMA((slots,)),
            pltpu.SemaphoreType.DMA((count,)),
            pltpu.SemaphoreType.DMA((count,)),
        ],
        compiler_params=pltpu.CompilerParams(collective_id=0, has_side_effects=True),
        name="gather",
    )(mid, line, burg, live_mask.reshape(1, seg), pair_list.reshape(13, 1, 1))
    eight = [a.reshape(3, 8, seg // 8) for a in (midpoints, line_vectors, burgers)]
    out = pl.pallas_call(
        functools.partial(force_kernel, dims),
        out_shape=jax.ShapeDtypeStruct((3, 1, seg), F32),
        in_specs=[smem] + [vmem] * 6,
        out_specs=vmem,
        scratch_shapes=[
            pltpu.VMEM((8, seg), F32),
            pltpu.VMEM((16, seg), F32),
            pltpu.VMEM((128, seg), F32),
            pltpu.VMEM((seg, 128), BF16),
            pltpu.VMEM((48, seg), BF16),
            pltpu.VMEM((48, seg), BF16),
            pltpu.VMEM((seg, 128), F32),
            pltpu.VMEM((kcount, 1, 128), F32),
            pltpu.SMEM((kcount, 1, 128), F32),
            pltpu.SemaphoreType.DMA,
        ],
        name="forces",
    )(ctrl, blocks, ctrl, *eight, live_mask.reshape(8, seg // 8))
    return out.reshape(3, 1, 1, 1, seg)


def solution(mesh):
    dims = tuple(mesh.shape[a] for a in AXES)
    placed = (
        P(None, "gx", "gy", "gz", None),
        P(None, "gx", "gy", "gz", None),
        P(None, "gx", "gy", "gz", None),
        P("gx", "gy", "gz", None),
        P(None, "gx", "gy", "gz"),
    )
    return jax.shard_map(
        functools.partial(on_device, dims),
        mesh=mesh,
        in_specs=placed,
        out_specs=P(None, "gx", "gy", "gz", None),
        check_vma=False,
    )
```
